256 devices in a mesh: occ: 16 (over z, y_hi), aux: 16 (over y_lo, x, core).
Axes of the slice: x: 4, y: 4 (y_hi: 2, y_lo: 2; y = y_hi * 2 + y_lo), z: 8, core: 2. Of those that a mesh axis runs over, the one named last changes fastest.
Arguments:
- orbital_b: bfloat16 [128, 3072, 768], P('occ', 'aux'), may hold values from -0.75 to 0.75
- occ_energy: float32 [128], replicated, may hold values from -3 to -0.5
- vir_energy: float32 [768], replicated, may hold values from 0.2 to 3
Outputs:
- gradient_term: bfloat16 [128, 3072, 768], P('occ', 'aux')
The draws below stay inside these ranges and needn't reach their ends.
All inputs are finite; a program needn't handle non-finite values.
Results may differ from the reference program's by a relative error of at most 0.0044.
Values may be sent and summed in bfloat16 or wider, within the bound.
A program may use at most 64 MiB of HBM per device.

```python
import jax
import jax.numpy as jnp
from jax import lax

I_DEV = 8
VIR = 768
NAUX = 3072
OCC = 128
N_OCC = 16


def level_of(key, dims, pieces, least, largest):
    def one(axis_at, parts):
        steps = jax.random.uniform(jax.random.fold_in(jax.random.fold_in(key, 6), axis_at), (parts,), jnp.float32, least / len(pieces), largest / len(pieces))
        return jnp.repeat(jnp.exp(steps), dims[axis_at] // parts).reshape((-1,) + (1,) * (len(dims) - axis_at - 1))

    loudness = one(*pieces[0])
    for cut in pieces[1:]:
        loudness = loudness * one(*cut)
    return loudness


def scatter_about(rng, dims, deviation, bound, shards=(), dtype=jnp.bfloat16):
    values = deviation * jax.random.normal(rng, dims, jnp.float32)
    if shards:
        values = values * level_of(rng, dims, shards, -0.22, 0.18)
    return jnp.clip(values, -bound, bound).astype(dtype)


def setup_inputs(seed: int = 0) -> dict:
    splits = jax.random.split(jax.random.key(seed), 4)
    return {
        "orbital_b": scatter_about(splits[0], (OCC, NAUX, VIR), (NAUX ** -0.25), 0.75, ((0, 16), (1, 16))),
        "occ_energy": jnp.clip(jax.random.uniform(splits[1], (OCC,), jnp.float32, -3.0, -0.5), -3.0, -0.5),
        "vir_energy": jnp.clip(jax.random.uniform(splits[2], (VIR,), jnp.float32, 0.2, 3.0), 0.2, 3.0),
    }


def reference(orbital_b, occ_energy, vir_energy):
    leaders = orbital_b[::I_DEV]
    zero_block = jnp.zeros_like(leaders[:1])
    before = jnp.concatenate([zero_block, leaders[:-1]], axis=0)
    follow = jnp.concatenate([leaders[1:], zero_block], axis=0)
    partner_b = jnp.stack([before, follow], axis=1)
    leader_energy = occ_energy[::I_DEV]
    energy_before = jnp.concatenate([leader_energy[:1], leader_energy[:-1]])
    energy_follow = jnp.concatenate([leader_energy[1:], leader_energy[-1:]])
    partner_energy = jnp.stack([energy_before, energy_follow], axis=1)
    blocks = orbital_b.reshape(N_OCC, I_DEV, NAUX, VIR)
    block_energy = occ_energy.reshape(N_OCC, I_DEV)

    def per_block(packed):
        block, energy, partners, pair_energy = packed
        block_wide = block.astype(jnp.float32)
        partner_wide = partners.astype(jnp.float32)
        integral = jnp.einsum("iPa,pPb->iapb", block_wide, partner_wide, precision=lax.Precision.HIGHEST)
        denominator = (vir_energy[None, :, None, None] + vir_energy[None, None, None, :]
                       - energy[:, None, None, None] - pair_energy[None, None, :, None])
        amplitude = (integral / denominator).astype(jnp.bfloat16)
        result = jnp.einsum("iapb,pPb->iPa", amplitude.astype(jnp.float32), partner_wide, precision=lax.Precision.HIGHEST)
        return result.astype(jnp.bfloat16)

    output = lax.map(per_block, (blocks, block_energy, partner_b, partner_energy))
    return output.reshape(N_OCC * I_DEV, NAUX, VIR)
```

```python
import functools

import jax
import jax.numpy as jnp
from jax import lax
from jax.experimental import pallas as pl
from jax.experimental.pallas import tpu as pltpu
from jax.sharding import PartitionSpec as P

MESH = pl.DeviceIdType.MESH
OFFSETS = ((0, 1), (0, 3), (1, 0), (0, 2), (1, 1), (1, 3), (1, 2))
ALONG_X = (1, 3, 2)
CHUNKS = 3


def kernel(planes, occ_e, vir, b_own, out, part, amp, gam, lead, b_in, b_t, integral, p_out, p_in,
           ls, lr, bs, br, ps, pr, as_, ar, gs, gr, local):
    rows, width = b_own.shape[1], b_own.shape[2]
    w = width // CHUNKS
    half = w // 2
    occ, aux = lax.axis_index("occ"), lax.axis_index("aux")
    z, yh = occ // 2, occ % 2
    yl, x, h = aux // 8, (aux // 2) % 4, aux % 2
    me = yl * 4 + x

    def device(z_to, yh_to, yl_to, x_to, h_to):
        return (lax.rem(z_to + planes, planes) * 2 + yh_to, (yl_to * 4 + x_to) * 2 + h_to)

    def chip(dy, dx):
        return lax.rem(yl + dy, 2), lax.rem(x + dx, 4)

    def send(src, dst, ssem, rsem, to):
        copy = pltpu.make_async_remote_copy(
            src_ref=src, dst_ref=dst, send_sem=ssem, recv_sem=rsem, device_id=to, device_id_type=MESH)
        copy.start()
        return copy

    step = 1 - 2 * yh
    twins = (device(z + step, yh, yl, x, h), device(z - step, yh, yl, x, h))
    mate = device(z, yh, yl, x, 1 - h)
    peers = []
    for dy, dx in OFFSETS:
        yp, xp = chip(dy, dx)
        peers.append(device(z, yh, yp, xp, h))
    sources = (device(z, 1 - yh, 0, x, h), device(z - step, 1 - yh, 1, x, h))
    z_col = z - yl * step
    columns = (device(z_col, 1 - yh, 0, x, h), device(z_col, 1 - yh, 1, x, h))

    barrier = pltpu.get_barrier_semaphore()
    for to in (*peers, mate, *twins, *sources):
        pl.semaphore_signal(barrier, inc=1, device_id=to, device_id_type=MESH)
    pl.semaphore_wait(barrier, 12)

    def span(c):
        return pl.ds(pl.multiple_of(c * rows, rows), rows)

    def cols(q):
        return pl.ds(q * w, w)

    waits = []

    def send_b(q):
        for n, (dy, dx) in enumerate(OFFSETS):
            yp, xp = chip(dy, dx)
            waits.append(send(b_own.at[yp * 4 + xp, :, cols(q)], b_in.at[span(me), cols(q)],
                              bs.at[q, n], br.at[q, n], peers[n]))

    for n in range(2):
        waits.append(send(b_own.at[0], lead.at[yl, span(me)], ls.at[0, n], lr.at[yl, 0], columns[n]))
    mine = pltpu.make_async_copy(b_own.at[me], b_in.at[span(me)], local.at[0])
    mine.start()
    send_b(0)

    def arrived(ref, sem):
        pltpu.make_async_copy(ref, ref, sem).wait()

    def piece(s, r):
        d = (0, *ALONG_X)[r]
        return s * 4 + lax.rem(x - d + 4, 4)

    for s in range(2):
        c = piece(s, 0)
        held = lead.at[s, span(c)]
        arrived(held, lr.at[s, 0])
        for n, d in enumerate(ALONG_X):
            waits.append(send(held, held, ls.at[1 + s, n], lr.at[s, 1 + n],
                              device(z, yh, yl, lax.rem(x + d, 4), h)))
        waits.append(send(held, lead.at[1 - s, span(c)], ls.at[3 + s, 0], lr.at[1 - s, 4], twins[s]))
    send_b(1)
    for r in range(1, 4):
        for s in range(2):
            c = piece(s, r)
            held = lead.at[s, span(c)]
            arrived(held, lr.at[s, r])
            waits.append(send(held, lead.at[1 - s, span(c)], ls.at[3 + s, r], lr.at[1 - s, 4 + r], twins[s]))
    send_b(2)
    mine.wait()
    for r in range(4):
        for s in range(2):
            arrived(lead.at[1 - s, span(piece(s, r))], lr.at[1 - s, 4 + r])

    z_b = z - step
    valid = jnp.where(jnp.logical_and(z_b >= 0, z_b < planes), 1.0, 0.0).astype(jnp.float32)
    block_b = jnp.clip(z_b, 0, planes - 1) * 2 + 1 - yh
    e_own = occ_e[occ * 8 + me]
    e_pair = (occ_e[(z * 2 + 1 - yh) * 8], occ_e[block_b * 8])

    own = pl.ds(pl.multiple_of(h * half, half), half)
    other = pl.ds(pl.multiple_of((1 - h) * half, half), half)

    def partial(q):
        for n, (dy, dx) in enumerate(OFFSETS):
            yp, xp = chip(-dy + 2, -dx + 4)
            arrived(b_in.at[span(yp * 4 + xp), cols(q)], br.at[q, n])
        b_t[...] = b_in[:, cols(q)].T
        for s in range(2):
            integral[:, s * width:(s + 1) * width] = jnp.dot(
                b_t[...], lead[s], preferred_element_type=jnp.float32)
        p_out[q] = integral[other, :].astype(jnp.bfloat16)
        waits.append(send(p_out.at[q], p_in.at[q], ps.at[q], pr.at[q], mate))

    def amplitude(q):
        arrived(p_in.at[q], pr.at[q])
        row = vir[0:1, pl.ds(pl.multiple_of(q * w + h * half, 128), half)]
        va = jnp.broadcast_to(row, (half, half)).T
        for s in range(2):
            for t in range(width // half):
                at = pl.ds(s * width + t * half, half)
                total = integral[own, at] + p_in[q, :, at].astype(jnp.float32)
                if s == 1:
                    total = total * valid
                low = va + vir[0:1, pl.ds(t * half, half)] - e_own - e_pair[s]
                amp[q, own, at] = (total / low).astype(jnp.bfloat16)
        waits.append(send(amp.at[q, own], amp.at[q, own], as_.at[q], ar.at[q], mate))

    def gamma(q):
        arrived(amp.at[q, other], ar.at[q])

        def one(c):
            acc = jnp.zeros((rows, w), jnp.float32)
            for s in range(2):
                acc += lax.dot_general(lead[s, span(c), :], amp[q, :, s * width:(s + 1) * width],
                                       (((1,), (1,)), ((), ())), preferred_element_type=jnp.float32)
            gam[q, span(c), :] = acc.astype(jnp.bfloat16)

        for n, (dy, dx) in enumerate(OFFSETS):
            yp, xp = chip(dy, dx)
            c = yp * 4 + xp
            one(c)
            waits.append(send(gam.at[q, span(c)], out.at[me, :, cols(q)], gs.at[q, n], gr.at[q, n], peers[n]))
        one(me)
        copy = pltpu.make_async_copy(gam.at[q, span(me)], out.at[me, :, cols(q)], local.at[1 + q])
        copy.start()
        return copy

    copies = []
    for q in range(CHUNKS):
        partial(q)
        amplitude(q)
        copies.append(gamma(q))

    for copy in waits:
        copy.wait_send()
    for copy in copies:
        copy.wait()
    for q in range(CHUNKS):
        for n, (dy, dx) in enumerate(OFFSETS):
            yp, xp = chip(-dy + 2, -dx + 4)
            arrived(out.at[yp * 4 + xp, :, cols(q)], gr.at[q, n])


def solution(mesh):
    planes = mesh.shape["occ"] // 2

    def shards(orbital_b, occ_energy, vir_energy):
        orbitals, rows, width = orbital_b.shape
        w = width // CHUNKS
        aux = orbitals * rows
        dma = pltpu.SemaphoreType.DMA
        bf16, f32 = jnp.bfloat16, jnp.float32
        result = pl.pallas_call(
            functools.partial(kernel, planes),
            out_shape=jax.ShapeDtypeStruct(orbital_b.shape, orbital_b.dtype),
            in_specs=[pl.BlockSpec(memory_space=pltpu.SMEM), pl.BlockSpec(memory_space=pltpu.VMEM),
                      pl.BlockSpec(memory_space=pl.ANY)],
            out_specs=pl.BlockSpec(memory_space=pl.ANY),
            scratch_shapes=[
                pltpu.VMEM((8, 128), f32),
                pltpu.VMEM((CHUNKS, w, 2 * width), bf16),
                pltpu.VMEM((CHUNKS, aux, w), bf16),
                pltpu.VMEM((2, aux, width), bf16),
                pltpu.VMEM((aux, width), bf16),
                pltpu.VMEM((w, aux), bf16),
                pltpu.VMEM((w, 2 * width), f32),
                pltpu.VMEM((CHUNKS, w // 2, 2 * width), bf16),
                pltpu.VMEM((CHUNKS, w // 2, 2 * width), bf16),
                dma((5, 4)), dma((2, 8)), dma((CHUNKS, 7)), dma((CHUNKS, 7)),
                dma((CHUNKS,)), dma((CHUNKS,)), dma((CHUNKS,)), dma((CHUNKS,)),
                dma((CHUNKS, 7)), dma((CHUNKS, 7)), dma((1 + CHUNKS,)),
            ],
            compiler_params=pltpu.CompilerParams(
                collective_id=0, has_side_effects=True, vmem_limit_bytes=48 * 2**20),
        )(occ_energy, vir_energy.reshape(1, -1), orbital_b)
        return result

    placed = (P("occ", "aux", None), P(), P())
    return jax.shard_map(
        shards, mesh=mesh, in_specs=placed, out_specs=P("occ", "aux", None), check_vma=False)
```

```python
import functools

import jax
import jax.numpy as jnp
from jax import lax
from jax.experimental import pallas as pl
from jax.experimental.pallas import tpu as pltpu
from jax.sharding import PartitionSpec as P

MESH = pl.DeviceIdType.MESH
OFFSETS = ((0, 1), (0, 3), (1, 0), (1, 1), (1, 3), (0, 2), (1, 2))
ALONG_X = (1, 3, 2)
CHUNKS = 3
PARTS = 4


def kernel(planes, occ_hbm, vir_hbm, b_own, out, occ_e, vir, vrow, scale, amp, gam, lead, b_in, b_t, integral,
           p_out, p_in, ls, lr, bs, br, ps, pr, as_, ar, gs, gr, local):
    rows, width = b_own.shape[1], b_own.shape[2]
    w = width // CHUNKS
    half = w // 2
    occ, aux = lax.axis_index("occ"), lax.axis_index("aux")
    z, yh = occ // 2, occ % 2
    yl, x, h = aux // 8, (aux // 2) % 4, aux % 2
    me = yl * 4 + x

    def device(z_to, yh_to, yl_to, x_to, h_to):
        return (lax.rem(z_to + planes, planes) * 2 + yh_to, (yl_to * 4 + x_to) * 2 + h_to)

    def chip(dy, dx):
        return lax.rem(yl + dy, 2), lax.rem(x + dx, 4)

    def send(src, dst, ssem, rsem, to):
        copy = pltpu.make_async_remote_copy(
            src_ref=src, dst_ref=dst, send_sem=ssem, recv_sem=rsem, device_id=to, device_id_type=MESH)
        copy.start()
        return copy

    step = 1 - 2 * yh
    twins = (device(z + step, yh, yl, x, h), device(z - step, yh, yl, x, h))
    mate = device(z, yh, yl, x, 1 - h)
    across = device(z, yh, 1 - yl, x, h)
    beside = [device(z, yh, yl, lax.rem(x + d, 4), h) for d in ALONG_X]
    far = (1 - yl) * 4 + x
    peers = []
    for dy, dx in OFFSETS:
        yp, xp = chip(dy, dx)
        peers.append(device(z, yh, yp, xp, h))
    column = device(z - yl * step, 1 - yh, 1 - yl, x, h)
    source = device(z - (1 - yl) * step, 1 - yh, 1 - yl, x, h)

    occ_in = pltpu.make_async_copy(occ_hbm, occ_e, local.at[1])
    vir_in = pltpu.make_async_copy(vir_hbm, vir, local.at[2])
    occ_in.start()
    vir_in.start()
    barrier = pltpu.get_barrier_semaphore()
    for to in (*peers, mate, *twins, source):
        pl.semaphore_signal(barrier, inc=1, device_id=to, device_id_type=MESH)
    pl.semaphore_wait(barrier, 11)

    def span(c):
        return pl.ds(pl.multiple_of(c * rows, rows), rows)

    def cols(q):
        return pl.ds(q * w, w)

    waits = []

    def send_b(q, which):
        for n in which:
            dy, dx = OFFSETS[n]
            yp, xp = chip(dy, dx)
            waits.append(send(b_own.at[yp * 4 + xp, :, cols(q)], b_in.at[span(me), cols(q)],
                              bs.at[q, n], br.at[q, n], peers[n]))

    def b_wait(q):
        for n, (dy, dx) in enumerate(OFFSETS):
            yp, xp = chip(-dy + 2, -dx + 4)
            arrived(b_in.at[span(yp * 4 + xp), cols(q)], br.at[q, n])

    fine = rows // PARTS

    def sub(c, t):
        return pl.ds(pl.multiple_of(c * rows + t * fine, fine), fine)

    def arrived(ref, sem):
        pltpu.make_async_copy(ref, ref, sem).wait()

    def piece(s, r):
        d = (0, *ALONG_X)[r]
        return s * 4 + lax.rem(x - d + 4, 4)

    def forward_x(s, c, t):
        held = lead.at[s, sub(c, t)]
        for n in range(2):
            waits.append(send(held, held, ls.at[1 + s, n, t], lr.at[s, 1 + n, t], beside[n]))

    def forward_z(s, c, r, t):
        to = device(z + (1 - 2 * s) * step, yh, yl, x, h)
        waits.append(send(lead.at[s, sub(c, t)], lead.at[1 - s, sub(c, t)], ls.at[3 + s, r, t],
                          lr.at[1 - s, 4 + r, t], to))

    z_b = z - step
    valid = jnp.where(jnp.logical_and(z_b >= 0, z_b < planes), 1.0, 0.0).astype(jnp.float32)
    block_b = jnp.clip(z_b, 0, planes - 1) * 2 + 1 - yh

    own = pl.ds(pl.multiple_of(h * half, half), half)
    other = pl.ds(pl.multiple_of((1 - h) * half, half), half)

    def scales(q):
        e_own = occ_e[occ * 8 + me]
        e_pair = (occ_e[(z * 2 + 1 - yh) * 8], occ_e[block_b * 8])
        va = jnp.broadcast_to(vrow[0:1, pl.ds(pl.multiple_of(q * w + h * half, 128), half)], (half, half)).T
        for s in range(2):
            for t in range(width // half):
                low = va + vrow[0:1, pl.ds(t * half, half)] - e_own - e_pair[s]
                scale[q, :, pl.ds(s * width + t * half, half)] = (valid if s else 1.0) / low

    for t in range(PARTS):
        waits.append(send(b_own.at[0, pl.ds(t * fine, fine)], lead.at[yl, sub(me, t)],
                          ls.at[0, 0, t], lr.at[yl, 0, t], column))
    send_b(0, range(3))
    mine = pltpu.make_async_copy(b_own.at[me], b_in.at[span(me)], local.at[0])
    mine.start()

    occ_in.wait()
    vir_in.wait()
    for t in range(width // half):
        vrow[0:1, pl.ds(t * half, half)] = vir[pl.ds(t * half, half)].reshape(1, half)

    for t in range(PARTS + 2):
        if t < PARTS:
            first = lead.at[1 - yl, sub(far, t)]
            arrived(first, lr.at[1 - yl, 0, t])
            waits.append(send(first, first, ls.at[0, 1, t], lr.at[1 - yl, 0, t], across))
            forward_x(1 - yl, far, t)
            forward_z(1 - yl, far, 0, t)
            arrived(lead.at[yl, sub(me, t)], lr.at[yl, 0, t])
            forward_x(yl, me, t)
            forward_z(yl, me, 0, t)
        if t < CHUNKS:
            scales(t)
        if t == PARTS - 1:
            send_b(0, range(3, 7))
        for r, lag in ((1, 1), (2, 1), (3, 2)):
            if r == 3 and t == PARTS:
                for q in range(1, CHUNKS):
                    send_b(q, range(7))
            if 0 <= t - lag < PARTS:
                u = t - lag
                for s in range(2):
                    c = piece(s, r)
                    arrived(lead.at[s, sub(c, u)], lr.at[s, r, u])
                    if r - 1 == u % 2:
                        held = lead.at[s, sub(c, u)]
                        waits.append(send(held, held, ls.at[1 + s, 2, u], lr.at[s, 3, u], beside[r - 1]))
                    forward_z(s, c, r, u)
    mine.wait()
    for t in range(PARTS):
        for r in range(4):
            for s in range(2):
                arrived(lead.at[1 - s, sub(piece(s, r), t)], lr.at[1 - s, 4 + r, t])

    def partial(q):
        b_wait(q)
        b_t[...] = b_in[:, cols(q)].T
        for s in range(2):
            integral[:, s * width:(s + 1) * width] = jnp.dot(
                b_t[...], lead[s], preferred_element_type=jnp.float32)
        p_out[q] = integral[other, :].astype(jnp.bfloat16)
        waits.append(send(p_out.at[q], p_in.at[q], ps.at[q], pr.at[q], mate))

    def amplitude(q):
        arrived(p_in.at[q], pr.at[q])
        for s in range(2):
            at = pl.ds(s * width, width)
            total = integral[own, at] + p_in[q, :, at].astype(jnp.float32)
            amp[q, own, at] = (total * scale[q, :, at]).astype(jnp.bfloat16)
        waits.append(send(amp.at[q, own], amp.at[q, own], as_.at[q], ar.at[q], mate))

    def gamma(q):
        arrived(amp.at[q, other], ar.at[q])

        def one(c):
            acc = jnp.zeros((rows, w), jnp.float32)
            for s in range(2):
                acc += lax.dot_general(lead[s, span(c), :], amp[q, :, s * width:(s + 1) * width],
                                       (((1,), (1,)), ((), ())), preferred_element_type=jnp.float32)
            gam[q, span(c), :] = acc.astype(jnp.bfloat16)

        for n, (dy, dx) in enumerate(OFFSETS):
            yp, xp = chip(dy, dx)
            c = yp * 4 + xp
            one(c)
            waits.append(send(gam.at[q, span(c)], out.at[me, :, cols(q)], gs.at[q, n], gr.at[q, n], peers[n]))
        one(me)
        copy = pltpu.make_async_copy(gam.at[q, span(me)], out.at[me, :, cols(q)], local.at[3 + q])
        copy.start()
        return copy

    copies = []
    partial(0)
    amplitude(0)
    copies.append(gamma(0))
    partial(1)
    for q in range(1, CHUNKS):
        amplitude(q)
        if q + 1 < CHUNKS:
            partial(q + 1)
        copies.append(gamma(q))

    for copy in waits:
        copy.wait_send()
    for copy in copies:
        copy.wait()
    for q in range(CHUNKS):
        for n, (dy, dx) in enumerate(OFFSETS):
            yp, xp = chip(-dy + 2, -dx + 4)
            arrived(out.at[yp * 4 + xp, :, cols(q)], gr.at[q, n])


def solution(mesh):
    planes = mesh.shape["occ"] // 2

    def shards(orbital_b, occ_energy, vir_energy):
        orbitals, rows, width = orbital_b.shape
        w = width // CHUNKS
        aux = orbitals * rows
        dma = pltpu.SemaphoreType.DMA
        bf16, f32 = jnp.bfloat16, jnp.float32
        result = pl.pallas_call(
            functools.partial(kernel, planes),
            out_shape=jax.ShapeDtypeStruct(orbital_b.shape, orbital_b.dtype),
            in_specs=[pl.BlockSpec(memory_space=pltpu.MemorySpace.HBM)] * 3,
            out_specs=pl.BlockSpec(memory_space=pl.ANY),
            scratch_shapes=[
                pltpu.SMEM(occ_energy.shape, f32),
                pltpu.VMEM(vir_energy.shape, f32),
                pltpu.VMEM((8, width), f32),
                pltpu.VMEM((CHUNKS, w // 2, 2 * width), f32),
                pltpu.VMEM((CHUNKS, w, 2 * width), bf16),
                pltpu.VMEM((CHUNKS, aux, w), bf16),
                pltpu.VMEM((2, aux, width), bf16),
                pltpu.VMEM((aux, width), bf16),
                pltpu.VMEM((w, aux), bf16),
                pltpu.VMEM((w, 2 * width), f32),
                pltpu.VMEM((CHUNKS, w // 2, 2 * width), bf16),
                pltpu.VMEM((CHUNKS, w // 2, 2 * width), bf16),
                dma((5, 4, PARTS)), dma((2, 8, PARTS)), dma((CHUNKS, 7)), dma((CHUNKS, 7)),
                dma((CHUNKS,)), dma((CHUNKS,)), dma((CHUNKS,)), dma((CHUNKS,)),
                dma((CHUNKS, 7)), dma((CHUNKS, 7)), dma((3 + CHUNKS,)),
            ],
            compiler_params=pltpu.CompilerParams(
                collective_id=0, has_side_effects=True, vmem_limit_bytes=48 * 2**20),
        )(occ_energy, vir_energy, orbital_b)
        return result

    placed = (P("occ", "aux", None), P(), P())
    return jax.shard_map(
        shards, mesh=mesh, in_specs=placed, out_specs=P("occ", "aux", None), check_vma=False)
```

```python
import functools

import jax
import jax.numpy as jnp
from jax import lax
from jax.experimental import pallas as pl
from jax.experimental.pallas import tpu as pltpu
from jax.sharding import PartitionSpec as P

MESH = pl.DeviceIdType.MESH
OFFSETS = ((0, 1), (0, 3), (1, 0), (0, 2), (1, 1), (1, 3), (1, 2))
ALONG_X = (1, 3, 2)
CHUNKS = 3
PARTS = 4


def kernel(planes, occ_hbm, vir_hbm, b_own, out, occ_e, vir, vrow, vcol, scale, amp, gam, lead, b_in, b_t, integral,
           p_out, p_in, ls, lr, bs, br, ps, pr, as_, ar, gs, gr, local):
    rows, width = b_own.shape[1], b_own.shape[2]
    w = width // CHUNKS
    half = w // 2
    occ, aux = lax.axis_index("occ"), lax.axis_index("aux")
    z, yh = occ // 2, occ % 2
    yl, x, h = aux // 8, (aux // 2) % 4, aux % 2
    me = yl * 4 + x

    def device(z_to, yh_to, yl_to, x_to, h_to):
        return (z_to * 2 + yh_to, (yl_to * 4 + x_to) * 2 + h_to)

    def within(z_to):
        return jnp.logical_and(z_to >= 0, z_to < planes)

    def chip(dy, dx):
        return lax.rem(yl + dy, 2), lax.rem(x + dx, 4)

    def send(src, dst, ssem, rsem, to):
        copy = pltpu.make_async_remote_copy(
            src_ref=src, dst_ref=dst, send_sem=ssem, recv_sem=rsem, device_id=to, device_id_type=MESH)
        copy.start()
        return copy

    step = 1 - 2 * yh

    def twin(s):
        z_to = z + (1 - 2 * s) * step
        inside = within(z_to)
        return device(jnp.where(inside, z_to, z), jnp.where(inside, yh, 1 - yh), jnp.where(inside, yl, 1 - yl), x, h)

    def entry(z_to):
        inside = within(z_to)
        return device(jnp.where(inside, z_to, z), jnp.where(inside, 1 - yh, yh), 1 - yl, x, h)

    twins = (twin(0), twin(1))
    mate = device(z, yh, yl, x, 1 - h)
    across = device(z, yh, 1 - yl, x, h)
    beside = [device(z, yh, yl, lax.rem(x + d, 4), h) for d in ALONG_X]
    far = (1 - yl) * 4 + x
    peers = []
    for dy, dx in OFFSETS:
        yp, xp = chip(dy, dx)
        peers.append(device(z, yh, yp, xp, h))
    column = entry(z - yl * step)
    source = entry(z - (1 - yl) * step)

    occ_in = pltpu.make_async_copy(occ_hbm, occ_e, local.at[1])
    vir_in = pltpu.make_async_copy(vir_hbm, vir, local.at[2])
    occ_in.start()
    vir_in.start()
    barrier = pltpu.get_barrier_semaphore()
    for to in (*peers, mate, *twins, source):
        pl.semaphore_signal(barrier, inc=1, device_id=to, device_id_type=MESH)
    pl.semaphore_wait(barrier, 11)

    def span(c):
        return pl.ds(pl.multiple_of(c * rows, rows), rows)

    def cols(q):
        return pl.ds(q * w, w)

    waits = []

    def send_b(q, which):
        for n in which:
            dy, dx = OFFSETS[n]
            yp, xp = chip(dy, dx)
            waits.append(send(b_own.at[yp * 4 + xp, :, cols(q)], b_in.at[span(me), cols(q)],
                              bs.at[q, n], br.at[q, n], peers[n]))

    def b_wait(q):
        for n, (dy, dx) in enumerate(OFFSETS):
            yp, xp = chip(-dy + 2, -dx + 4)
            arrived(b_in.at[span(yp * 4 + xp), cols(q)], br.at[q, n])

    fine = rows // PARTS

    def sub(c, t):
        return pl.ds(pl.multiple_of(c * rows + t * fine, fine), fine)

    def arrived(ref, sem):
        pltpu.make_async_copy(ref, ref, sem).wait()

    def piece(s, r):
        d = (0, *ALONG_X)[r]
        return s * 4 + lax.rem(x - d + 4, 4)

    def forward_x(s, c, t):
        held = lead.at[s, sub(c, t)]
        for n in range(2):
            waits.append(send(held, held, ls.at[1 + s, n, t], lr.at[s, 1 + n, t], beside[n]))

    def forward_z(s, c, r, t):
        to = twin(s)
        waits.append(send(lead.at[s, sub(c, t)], lead.at[1 - s, sub(c, t)], ls.at[3 + s, r, t],
                          lr.at[1 - s, 4 + r, t], to))

    z_b = z - step
    valid = jnp.where(within(z_b), 1.0, 0.0).astype(jnp.float32)
    block_b = jnp.clip(z_b, 0, planes - 1) * 2 + 1 - yh

    own = pl.ds(pl.multiple_of(h * half, half), half)
    other = pl.ds(pl.multiple_of((1 - h) * half, half), half)

    def scales(q):
        e_own = occ_e[occ * 8 + me]
        e_pair = (occ_e[(z * 2 + 1 - yh) * 8], occ_e[block_b * 8])
        for u in range(w // 128):
            column_of = jnp.broadcast_to(vrow[0:1, pl.ds(q * w + u * 128, 128)], (128, 128))
            vcol[pl.ds(u * 128, 128), :] = column_of.T
        va = vcol[own, :]
        for s in range(2):
            for t in range(width // 128):
                low = va + vrow[0:1, pl.ds(t * 128, 128)] - e_own - e_pair[s]
                scale[q, :, pl.ds(s * width + t * 128, 128)] = (valid if s else 1.0) / low

    def enter(t):
        waits.append(send(b_own.at[0, pl.ds(t * fine, fine)], lead.at[yl, sub(me, t)],
                          ls.at[0, 0, t], lr.at[yl, 0, t], column))

    enter(0)
    enter(1)
    send_b(0, range(3))
    mine = pltpu.make_async_copy(b_own.at[me], b_in.at[span(me)], local.at[0])
    mine.start()

    occ_in.wait()
    vir_in.wait()
    for t in range(width // 128):
        vrow[0:1, pl.ds(t * 128, 128)] = vir[pl.ds(t * 128, 128)].reshape(1, 128)

    for t in range(PARTS + 2):
        if t < PARTS:
            first = lead.at[1 - yl, sub(far, t)]
            arrived(first, lr.at[1 - yl, 0, t])
            waits.append(send(first, first, ls.at[0, 1, t], lr.at[1 - yl, 0, t], across))
            forward_x(1 - yl, far, t)
            forward_z(1 - yl, far, 0, t)
            arrived(lead.at[yl, sub(me, t)], lr.at[yl, 0, t])
            forward_x(yl, me, t)
            forward_z(yl, me, 0, t)
        if t + 2 < PARTS:
            enter(t + 2)
        if t < CHUNKS:
            scales(t)
        if t == PARTS - 1:
            send_b(0, range(3, 7))
        for r, lag in ((1, 1), (2, 1), (3, 2)):
            if r == 3 and t == PARTS:
                for q in range(1, CHUNKS):
                    send_b(q, range(7))
            if 0 <= t - lag < PARTS:
                u = t - lag
                for s in range(2):
                    c = piece(s, r)
                    arrived(lead.at[s, sub(c, u)], lr.at[s, r, u])
                    if r - 1 == u % 2:
                        held = lead.at[s, sub(c, u)]
                        waits.append(send(held, held, ls.at[1 + s, 2, u], lr.at[s, 3, u], beside[r - 1]))
                    forward_z(s, c, r, u)
    mine.wait()
    for t in range(PARTS):
        for r in range(4):
            for s in range(2):
                arrived(lead.at[1 - s, sub(piece(s, r), t)], lr.at[1 - s, 4 + r, t])

    def partial(q):
        b_wait(q)
        b_t[...] = b_in[:, cols(q)].T
        for s in range(2):
            integral[:, s * width:(s + 1) * width] = jnp.dot(
                b_t[...], lead[s], preferred_element_type=jnp.float32)
        p_out[q] = integral[other, :].astype(jnp.bfloat16)
        waits.append(send(p_out.at[q], p_in.at[q], ps.at[q], pr.at[q], mate))

    def amplitude(q):
        arrived(p_in.at[q], pr.at[q])
        for s in range(2):
            at = pl.ds(s * width, width)
            total = integral[own, at] + p_in[q, :, at].astype(jnp.float32)
            amp[q, own, at] = (total * scale[q, :, at]).astype(jnp.bfloat16)
        waits.append(send(amp.at[q, own], amp.at[q, own], as_.at[q], ar.at[q], mate))

    def gamma(q):
        arrived(amp.at[q, other], ar.at[q])

        def one(c):
            acc = jnp.zeros((rows, w), jnp.float32)
            for s in range(2):
                acc += lax.dot_general(lead[s, span(c), :], amp[q, :, s * width:(s + 1) * width],
                                       (((1,), (1,)), ((), ())), preferred_element_type=jnp.float32)
            gam[q, span(c), :] = acc.astype(jnp.bfloat16)

        for n, (dy, dx) in enumerate(OFFSETS):
            yp, xp = chip(dy, dx)
            c = yp * 4 + xp
            one(c)
            waits.append(send(gam.at[q, span(c)], out.at[me, :, cols(q)], gs.at[q, n], gr.at[q, n], peers[n]))
        one(me)
        copy = pltpu.make_async_copy(gam.at[q, span(me)], out.at[me, :, cols(q)], local.at[3 + q])
        copy.start()
        return copy

    copies = []
    partial(0)
    amplitude(0)
    copies.append(gamma(0))
    partial(1)
    for q in range(1, CHUNKS):
        amplitude(q)
        if q + 1 < CHUNKS:
            partial(q + 1)
        copies.append(gamma(q))

    for copy in waits:
        copy.wait_send()
    for copy in copies:
        copy.wait()
    for q in range(CHUNKS):
        for n, (dy, dx) in enumerate(OFFSETS):
            yp, xp = chip(-dy + 2, -dx + 4)
            arrived(out.at[yp * 4 + xp, :, cols(q)], gr.at[q, n])


def solution(mesh):
    planes = mesh.shape["occ"] // 2

    def shards(orbital_b, occ_energy, vir_energy):
        orbitals, rows, width = orbital_b.shape
        w = width // CHUNKS
        aux = orbitals * rows
        dma = pltpu.SemaphoreType.DMA
        bf16, f32 = jnp.bfloat16, jnp.float32
        result = pl.pallas_call(
            functools.partial(kernel, planes),
            out_shape=jax.ShapeDtypeStruct(orbital_b.shape, orbital_b.dtype),
            in_specs=[pl.BlockSpec(memory_space=pltpu.MemorySpace.HBM)] * 3,
            out_specs=pl.BlockSpec(memory_space=pl.ANY),
            scratch_shapes=[
                pltpu.SMEM(occ_energy.shape, f32),
                pltpu.VMEM(vir_energy.shape, f32),
                pltpu.VMEM((8, width), f32),
                pltpu.VMEM((w, 128), f32),
                pltpu.VMEM((CHUNKS, w // 2, 2 * width), f32),
                pltpu.VMEM((CHUNKS, w, 2 * width), bf16),
                pltpu.VMEM((CHUNKS, aux, w), bf16),
                pltpu.VMEM((2, aux, width), bf16),
                pltpu.VMEM((aux, width), bf16),
                pltpu.VMEM((w, aux), bf16),
                pltpu.VMEM((w, 2 * width), f32),
                pltpu.VMEM((CHUNKS, w // 2, 2 * width), bf16),
                pltpu.VMEM((CHUNKS, w // 2, 2 * width), bf16),
                dma((5, 4, PARTS)), dma((2, 8, PARTS)), dma((CHUNKS, 7)), dma((CHUNKS, 7)),
                dma((CHUNKS,)), dma((CHUNKS,)), dma((CHUNKS,)), dma((CHUNKS,)),
                dma((CHUNKS, 7)), dma((CHUNKS, 7)), dma((3 + CHUNKS,)),
            ],
            compiler_params=pltpu.CompilerParams(
                collective_id=0, has_side_effects=True, vmem_limit_bytes=48 * 2**20),
        )(*(pltpu.with_memory_space_constraint(v, pltpu.MemorySpace.HBM) for v in (occ_energy, vir_energy, orbital_b)))
        return result

    placed = (P("occ", "aux", None), P(), P())
    return jax.shard_map(
        shards, mesh=mesh, in_specs=placed, out_specs=P("occ", "aux", None), check_vma=False)
```

```python
import functools

import jax
import jax.numpy as jnp
from jax import lax
from jax.experimental import pallas as pl
from jax.experimental.pallas import tpu as pltpu
from jax.sharding import PartitionSpec as P

MESH = pl.DeviceIdType.MESH
OFFSETS = ((0, 1), (0, 3), (1, 0), (0, 2), (1, 1), (1, 3), (1, 2))
ALONG_X = (1, 3, 2)
CHUNKS = 3
PARTS = 4


def kernel(planes, occ_hbm, vir_hbm, b_own, out, occ_e, vir, vrow, vcol, scale, amp, gam, lead, b_in, b_t, integral,
           p_out, p_in, ls, lr, bs, br, ps, pr, as_, ar, gs, gr, local):
    rows, width = b_own.shape[1], b_own.shape[2]
    w = width // CHUNKS
    half = w // 2
    occ, aux = lax.axis_index("occ"), lax.axis_index("aux")
    z, yh = occ // 2, occ % 2
    yl, x, h = aux // 8, (aux // 2) % 4, aux % 2
    me = yl * 4 + x

    def device(z_to, yh_to, yl_to, x_to, h_to):
        return (z_to * 2 + yh_to, (yl_to * 4 + x_to) * 2 + h_to)

    def within(z_to):
        return jnp.logical_and(z_to >= 0, z_to < planes)

    def chip(dy, dx):
        return lax.rem(yl + dy, 2), lax.rem(x + dx, 4)

    def send(src, dst, ssem, rsem, to):
        copy = pltpu.make_async_remote_copy(
            src_ref=src, dst_ref=dst, send_sem=ssem, recv_sem=rsem, device_id=to, device_id_type=MESH)
        copy.start()
        return copy

    step = 1 - 2 * yh

    def twin(s):
        z_to = z + (1 - 2 * s) * step
        inside = within(z_to)
        return device(jnp.where(inside, z_to, z), jnp.where(inside, yh, 1 - yh), jnp.where(inside, yl, 1 - yl), x, h)

    def entry(z_to):
        inside = within(z_to)
        return device(jnp.where(inside, z_to, z), jnp.where(inside, 1 - yh, yh), 1 - yl, x, h)

    twins = (twin(0), twin(1))
    mate = device(z, yh, yl, x, 1 - h)
    across = device(z, yh, 1 - yl, x, h)
    beside = [device(z, yh, yl, lax.rem(x + d, 4), h) for d in ALONG_X]
    far = (1 - yl) * 4 + x
    peers = []
    for dy, dx in OFFSETS:
        yp, xp = chip(dy, dx)
        peers.append(device(z, yh, yp, xp, h))
    column = entry(z - yl * step)
    source = entry(z - (1 - yl) * step)

    occ_in = pltpu.make_async_copy(occ_hbm, occ_e, local.at[1])
    vir_in = pltpu.make_async_copy(vir_hbm, vir, local.at[2])
    occ_in.start()
    vir_in.start()
    barrier = pltpu.get_barrier_semaphore()
    for to in (*peers, mate, *twins, source):
        pl.semaphore_signal(barrier, inc=1, device_id=to, device_id_type=MESH)
    pl.semaphore_wait(barrier, 11)

    def span(c):
        return pl.ds(pl.multiple_of(c * rows, rows), rows)

    def cols(q):
        return pl.ds(q * w, w)

    waits = []

    def send_b(q, which):
        for n in which:
            dy, dx = OFFSETS[n]
            yp, xp = chip(dy, dx)
            waits.append(send(b_own.at[yp * 4 + xp, :, cols(q)], b_in.at[span(me), cols(q)],
                              bs.at[q, n], br.at[q, n], peers[n]))

    def b_wait(q):
        for n, (dy, dx) in enumerate(OFFSETS):
            yp, xp = chip(-dy + 2, -dx + 4)
            arrived(b_in.at[span(yp * 4 + xp), cols(q)], br.at[q, n])

    fine = rows // PARTS

    def sub(c, t):
        return pl.ds(pl.multiple_of(c * rows + t * fine, fine), fine)

    def arrived(ref, sem):
        pltpu.make_async_copy(ref, ref, sem).wait()

    def piece(s, r):
        d = (0, *ALONG_X)[r]
        return s * 4 + lax.rem(x - d + 4, 4)

    def forward_x(s, c, t):
        held = lead.at[s, sub(c, t)]
        for n in range(2):
            waits.append(send(held, held, ls.at[1 + s, n, t], lr.at[s, 1 + n, t], beside[n]))

    def forward_z(s, c, r, t):
        to = twin(s)
        waits.append(send(lead.at[s, sub(c, t)], lead.at[1 - s, sub(c, t)], ls.at[3 + s, r, t],
                          lr.at[1 - s, 4 + r, t], to))

    z_b = z - step
    valid = jnp.where(within(z_b), 1.0, 0.0).astype(jnp.float32)
    block_b = jnp.clip(z_b, 0, planes - 1) * 2 + 1 - yh

    own = pl.ds(pl.multiple_of(h * half, half), half)
    other = pl.ds(pl.multiple_of((1 - h) * half, half), half)

    def scales(q):
        e_own = occ_e[occ * 8 + me]
        e_pair = (occ_e[(z * 2 + 1 - yh) * 8], occ_e[block_b * 8])
        for u in range(w // 128):
            column_of = jnp.broadcast_to(vrow[0:1, pl.ds(q * w + u * 128, 128)], (128, 128))
            vcol[pl.ds(u * 128, 128), :] = column_of.T
        va = vcol[own, :]
        for s in range(2):
            for t in range(width // 128):
                low = va + vrow[0:1, pl.ds(t * 128, 128)] - e_own - e_pair[s]
                scale[q, :, pl.ds(s * width + t * 128, 128)] = (valid if s else 1.0) / low

    def enter(t):
        waits.append(send(b_own.at[0, pl.ds(t * fine, fine)], lead.at[yl, sub(me, t)],
                          ls.at[0, 0, t], lr.at[yl, 0, t], column))

    enter(0)
    enter(1)
    send_b(0, range(4))
    mine = pltpu.make_async_copy(b_own.at[me], b_in.at[span(me)], local.at[0])
    mine.start()

    occ_in.wait()
    vir_in.wait()
    for t in range(width // 128):
        vrow[0:1, pl.ds(t * 128, 128)] = vir[pl.ds(t * 128, 128)].reshape(1, 128)

    for t in range(PARTS + 2):
        if t < PARTS:
            first = lead.at[1 - yl, sub(far, t)]
            arrived(first, lr.at[1 - yl, 0, t])
            waits.append(send(first, first, ls.at[0, 1, t], lr.at[1 - yl, 0, t], across))
            forward_x(1 - yl, far, t)
            forward_z(1 - yl, far, 0, t)
            arrived(lead.at[yl, sub(me, t)], lr.at[yl, 0, t])
            forward_x(yl, me, t)
            forward_z(yl, me, 0, t)
        if t + 2 < PARTS:
            enter(t + 2)
        if t < CHUNKS:
            scales(t)
        if t == PARTS - 1:
            send_b(0, range(4, 7))
        for r, lag in ((1, 1), (2, 1), (3, 2)):
            if r == 3 and t == PARTS:
                for q in range(1, CHUNKS):
                    send_b(q, range(7))
            if 0 <= t - lag < PARTS:
                u = t - lag
                for s in range(2):
                    c = piece(s, r)
                    arrived(lead.at[s, sub(c, u)], lr.at[s, r, u])
                    if r - 1 == u % 2:
                        held = lead.at[s, sub(c, u)]
                        waits.append(send(held, held, ls.at[1 + s, 2, u], lr.at[s, 3, u], beside[r - 1]))
                    forward_z(s, c, r, u)
    mine.wait()
    for t in range(PARTS):
        for r in range(4):
            for s in range(2):
                arrived(lead.at[1 - s, sub(piece(s, r), t)], lr.at[1 - s, 4 + r, t])

    def partial(q):
        b_wait(q)
        b_t[...] = b_in[:, cols(q)].T
        for s in range(2):
            integral[:, s * width:(s + 1) * width] = jnp.dot(
                b_t[...], lead[s], preferred_element_type=jnp.float32)
        p_out[q] = integral[other, :].astype(jnp.bfloat16)
        waits.append(send(p_out.at[q], p_in.at[q], ps.at[q], pr.at[q], mate))

    def amplitude(q):
        arrived(p_in.at[q], pr.at[q])
        for s in range(2):
            at = pl.ds(s * width, width)
            total = integral[own, at] + p_in[q, :, at].astype(jnp.float32)
            amp[q, own, at] = (total * scale[q, :, at]).astype(jnp.bfloat16)
        waits.append(send(amp.at[q, own], amp.at[q, own], as_.at[q], ar.at[q], mate))

    def gamma(q):
        arrived(amp.at[q, other], ar.at[q])

        def one(c):
            acc = jnp.zeros((rows, w), jnp.float32)
            for s in range(2):
                acc += lax.dot_general(lead[s, span(c), :], amp[q, :, s * width:(s + 1) * width],
                                       (((1,), (1,)), ((), ())), preferred_element_type=jnp.float32)
            gam[q, span(c), :] = acc.astype(jnp.bfloat16)

        for n, (dy, dx) in enumerate(OFFSETS):
            yp, xp = chip(dy, dx)
            c = yp * 4 + xp
            one(c)
            waits.append(send(gam.at[q, span(c)], out.at[me, :, cols(q)], gs.at[q, n], gr.at[q, n], peers[n]))
        one(me)
        copy = pltpu.make_async_copy(gam.at[q, span(me)], out.at[me, :, cols(q)], local.at[3 + q])
        copy.start()
        return copy

    copies = []
    partial(0)
    amplitude(0)
    copies.append(gamma(0))
    partial(1)
    for q in range(1, CHUNKS):
        amplitude(q)
        if q + 1 < CHUNKS:
            partial(q + 1)
        copies.append(gamma(q))

    for copy in waits:
        copy.wait_send()
    for copy in copies:
        copy.wait()
    for q in range(CHUNKS):
        for n, (dy, dx) in enumerate(OFFSETS):
            yp, xp = chip(-dy + 2, -dx + 4)
            arrived(out.at[yp * 4 + xp, :, cols(q)], gr.at[q, n])


def solution(mesh):
    planes = mesh.shape["occ"] // 2

    def shards(orbital_b, occ_energy, vir_energy):
        orbitals, rows, width = orbital_b.shape
        w = width // CHUNKS
        aux = orbitals * rows
        dma = pltpu.SemaphoreType.DMA
        bf16, f32 = jnp.bfloat16, jnp.float32
        result = pl.pallas_call(
            functools.partial(kernel, planes),
            out_shape=jax.ShapeDtypeStruct(orbital_b.shape, orbital_b.dtype),
            in_specs=[pl.BlockSpec(memory_space=pltpu.MemorySpace.HBM)] * 3,
            out_specs=pl.BlockSpec(memory_space=pl.ANY),
            scratch_shapes=[
                pltpu.SMEM(occ_energy.shape, f32),
                pltpu.VMEM(vir_energy.shape, f32),
                pltpu.VMEM((8, width), f32),
                pltpu.VMEM((w, 128), f32),
                pltpu.VMEM((CHUNKS, w // 2, 2 * width), f32),
                pltpu.VMEM((CHUNKS, w, 2 * width), bf16),
                pltpu.VMEM((CHUNKS, aux, w), bf16),
                pltpu.VMEM((2, aux, width), bf16),
                pltpu.VMEM((aux, width), bf16),
                pltpu.VMEM((w, aux), bf16),
                pltpu.VMEM((w, 2 * width), f32),
                pltpu.VMEM((CHUNKS, w // 2, 2 * width), bf16),
                pltpu.VMEM((CHUNKS, w // 2, 2 * width), bf16),
                dma((5, 4, PARTS)), dma((2, 8, PARTS)), dma((CHUNKS, 7)), dma((CHUNKS, 7)),
                dma((CHUNKS,)), dma((CHUNKS,)), dma((CHUNKS,)), dma((CHUNKS,)),
                dma((CHUNKS, 7)), dma((CHUNKS, 7)), dma((3 + CHUNKS,)),
            ],
            compiler_params=pltpu.CompilerParams(
                collective_id=0, has_side_effects=True, vmem_limit_bytes=48 * 2**20),
        )(*(pltpu.with_memory_space_constraint(v, pltpu.MemorySpace.HBM) for v in (occ_energy, vir_energy, orbital_b)))
        return result

    placed = (P("occ", "aux", None), P(), P())
    return jax.shard_map(
        shards, mesh=mesh, in_specs=placed, out_specs=P("occ", "aux", None), check_vma=False)
```
